32 devices in a mesh: pipe: 4 (over y, core), tensor: 4 (over z), dp: 2 (over x).
Axes of the slice: x: 2, y: 2, z: 4, core: 2. Of those that a mesh axis runs over, the one named last changes fastest.
Arguments:
- out_grad: bfloat16 [4, 2, 128, 2560], P('pipe', 'dp', None, 'tensor'), may hold values from -6 to 6
- gate_pre: bfloat16 [4, 2, 13824, 128], P('pipe', 'dp', 'tensor'), may hold values from -6 to 6
- up_pre: bfloat16 [4, 2, 13824, 128], P('pipe', 'dp', 'tensor'), may hold values from -6 to 6
- down_weight: bfloat16 [4, 13824, 2560], P('pipe', 'tensor'), may hold values from -0.125 to 0.125
Outputs:
- gate_grad: bfloat16 [4, 2, 13824, 128], P('pipe', 'dp', 'tensor')
- up_grad: bfloat16 [4, 2, 13824, 128], P('pipe', 'dp', 'tensor')
- weight_grad: bfloat16 [4, 13824, 2560], P('pipe', 'tensor', 'dp')
The draws below stay inside these ranges and needn't reach their ends.
All inputs are finite; a program needn't handle non-finite values.
Results may differ from the reference program's by a relative error of at most 0.0075.
Values may be sent and summed in bfloat16 or wider, within the bound.
No kernel may reach another device: no remote copies, remote signals or barrier semaphores. Data moves between devices by JAX's collectives and lax.ppermute only.
A program may use at most 64 MiB of HBM per device.

```python
import jax
import jax.numpy as jnp
from jax import lax

D_W = 2560
FF_W = 13824
TOK = 128
N_PIPE = 4
N_DP = 2


def block_scale(stream_key, dims, shards, low, top_value):
    gain, own = 1.0, jax.random.fold_in(stream_key, 6)
    for position, blocks in shards:
        draws = jnp.exp(jax.random.uniform(jax.random.fold_in(own, position), (blocks,), jnp.float32, low / len(shards), top_value / len(shards)))
        gain = gain * jnp.repeat(draws, dims[position] // blocks).reshape([-1 if axis == position else 1 for axis in range(len(dims))])
    return gain


def centred(stream_key, extent, scale, limit, cuts=(), kind=jnp.bfloat16):
    gain = block_scale(stream_key, extent, cuts, -0.22, 0.18) if cuts else 1.0
    array = jax.random.normal(stream_key, extent, jnp.float32) * scale * gain
    return jnp.minimum(jnp.maximum(array, -limit), limit).astype(kind)


def setup_inputs(seed: int = 0) -> dict:
    key_list = jax.random.split(jax.random.key(seed), 5)
    out_grad = centred(key_list[0], (N_PIPE, N_DP, TOK, D_W), 1.0, 6.0, ((0, 4), (1, 2), (3, 4)))
    gate_pre = centred(key_list[1], (N_PIPE, N_DP, FF_W, TOK), 1.0, 6.0, ((0, 4), (1, 2), (2, 4)))
    up_pre = centred(key_list[2], (N_PIPE, N_DP, FF_W, TOK), 1.0, 6.0, ((0, 4), (1, 2), (2, 4)))
    down_weight = centred(key_list[3], (N_PIPE, FF_W, D_W), D_W ** -0.5, 0.125, ((0, 4), (1, 4)))
    return {"out_grad": out_grad, "gate_pre": gate_pre, "up_pre": up_pre, "down_weight": down_weight}


def section_grads(inputs):
    grad_out, gate_in, up_in, weight = inputs
    gate_vals = gate_in.astype(jnp.float32)
    up_vals = up_in.astype(jnp.float32)
    sigmoid_gate = jax.nn.sigmoid(gate_vals)
    silu_gate = gate_vals * sigmoid_gate
    hidden = (silu_gate * up_vals).astype(jnp.bfloat16)
    hidden_grad = jnp.einsum("fd,rtd->rft", weight.astype(jnp.float32), grad_out.astype(jnp.float32))
    gate_grad = (hidden_grad * up_vals * sigmoid_gate * (1.0 + gate_vals * (1.0 - sigmoid_gate))).astype(jnp.bfloat16)
    up_grad = (hidden_grad * silu_gate).astype(jnp.bfloat16)
    replica_sum = jnp.einsum("rft,rtd->fd", hidden.astype(jnp.float32), grad_out.astype(jnp.float32))
    return gate_grad, up_grad, replica_sum.astype(jnp.bfloat16)


def reference(out_grad, gate_pre, up_pre, down_weight):
    gate_grad, up_grad, pair_term = lax.map(section_grads, (out_grad, gate_pre, up_pre, down_weight))
    partner_term = jnp.roll(pair_term, N_PIPE // 2, axis=0)
    grad_scale = 32.0 / (2.0 * N_DP * TOK)
    weight_grad = ((pair_term.astype(jnp.float32) + partner_term.astype(jnp.float32)) * grad_scale).astype(jnp.bfloat16)
    return (gate_grad, up_grad, weight_grad)
```

```python
import jax
import jax.numpy as jnp
from jax import lax
from jax.sharding import PartitionSpec as P


def shifted(value, axis, step):
    size = lax.axis_size(axis)
    return lax.ppermute(value, axis, [(i, (i + step) % size) for i in range(size)])


def mirrored(value):
    half = lax.axis_size("pipe") // 2
    return lax.ppermute(value, "pipe", [(i, i ^ half) for i in range(2 * half)])


def on_device(out_grad, gate_pre, up_pre, down_weight):
    n_dp = lax.axis_size("dp")
    n_tensor = lax.axis_size("tensor")
    own_grad = out_grad[0, 0]
    tokens, shard = own_grad.shape
    width = shard * n_tensor
    block = width // n_dp
    rows = gate_pre.shape[2]
    pieces = 3
    chunk = rows // pieces
    z = lax.axis_index("tensor")
    x = lax.axis_index("dp")

    grad_full = jnp.zeros((tokens, width), jnp.bfloat16)
    grad_full = lax.dynamic_update_slice(grad_full, own_grad, (0, z * shard))
    for step in range(1, n_tensor):
        got = shifted(own_grad, "tensor", step)
        grad_full = lax.dynamic_update_slice(
            grad_full, got, (0, (z - step) % n_tensor * shard)
        )

    gate = gate_pre[0, 0].astype(jnp.float32)
    up = up_pre[0, 0].astype(jnp.float32)
    sig = jax.nn.sigmoid(gate)
    hidden = (gate * sig * up).astype(jnp.bfloat16)
    hid = [hidden[i * chunk : (i + 1) * chunk] for i in range(pieces)]
    hid_y = [mirrored(h) for h in hid]
    hid_x = [[shifted(h, "dp", s) for h in hid] for s in range(1, n_dp)]
    hid_d = [
        [
            mirrored(hid_x[s - 1][i]) if i == pieces - 1 else shifted(hid_y[i], "dp", s)
            for i in range(pieces)
        ]
        for s in range(1, n_dp)
    ]

    hidden_grad = lax.dot_general(
        down_weight[0], grad_full, (((1,), (1,)), ((), ())), preferred_element_type=jnp.float32
    )
    gate_grad = (hidden_grad * up * sig * (1.0 + gate * (1.0 - sig))).astype(jnp.bfloat16)
    up_grad = (hidden_grad * gate * sig).astype(jnp.bfloat16)

    def columns(target):
        return lax.dynamic_slice(grad_full, (0, target * block), (tokens, block))

    cols = [columns(x)]
    cols.append(mirrored(cols[0]))
    for s in range(1, n_dp):
        got = shifted(columns((x + s) % n_dp), "dp", s)
        cols += [got, mirrored(got)]
    cols = jnp.concatenate(cols, axis=0)
    scale = 32.0 / (2.0 * n_dp * tokens)
    out = []
    for i in range(pieces):
        parts = [hid[i], hid_y[i]]
        for s in range(1, n_dp):
            parts += [hid_x[s - 1][i], hid_d[s - 1][i]]
        total = jnp.dot(
            jnp.concatenate(parts, axis=1), cols, preferred_element_type=jnp.float32
        )
        out.append((total * scale).astype(jnp.bfloat16))
    weight_grad = jnp.concatenate(out, axis=0)
    return gate_grad[None, None], up_grad[None, None], weight_grad[None]


def solution(mesh):
    in_specs = (
        P("pipe", "dp", None, "tensor"),
        P("pipe", "dp", "tensor", None),
        P("pipe", "dp", "tensor", None),
        P("pipe", "tensor", None),
    )
    out_specs = (
        P("pipe", "dp", "tensor", None),
        P("pipe", "dp", "tensor", None),
        P("pipe", "tensor", "dp"),
    )
    return jax.shard_map(
        on_device, mesh=mesh, in_specs=in_specs, out_specs=out_specs, check_vma=False
    )
```

```python
import functools

import jax
import jax.numpy as jnp
from jax import lax
from jax.experimental import pallas as pl
from jax.experimental.pallas import tpu as pltpu
from jax.sharding import PartitionSpec as P


BF16 = jnp.bfloat16
F32 = jnp.float32


def shifted(value, axis, step):
    size = lax.axis_size(axis)
    return lax.ppermute(value, axis, [(i, (i + step) % size) for i in range(size)])


def crossed(value, axis, mask):
    return lax.ppermute(value, axis, [(i, i ^ mask) for i in range(lax.axis_size(axis))])


def mirrored(value):
    return crossed(value, "pipe", lax.axis_size("pipe") // 2)


def opposite(value):
    n_pipe, n_dp = lax.axis_size("pipe"), lax.axis_size("dp")
    mask = n_pipe // 2 * n_dp + 1
    return lax.ppermute(
        value, ("pipe", "dp"), [(i, i ^ mask) for i in range(n_pipe * n_dp)]
    )


HIDDEN_LIMIT = 60 << 20
LOAD_LIMIT = 30 << 20
GRADS_LIMIT = 6 << 20


def hidden_kernel(cuts, gate_hbm, up_hbm, *refs):
    outs, (gate, up, sems) = refs[:-3], refs[-3:]
    copies = []
    for k, (start, count) in enumerate(cuts[2:]):
        part = pl.ds(start, count)
        pair = [
            pltpu.make_async_copy(gate_hbm.at[0, 0, part], gate.at[part], sems.at[0, k]),
            pltpu.make_async_copy(up_hbm.at[0, 0, part], up.at[part], sems.at[1, k]),
        ]
        for copy in pair:
            copy.start()
        copies.append(pair)
    for (start, count), pair, out in zip(cuts[2:], copies, outs[2:]):
        for copy in pair:
            copy.wait()
        g = gate[start : start + count].astype(F32)
        u = up[start : start + count].astype(F32)
        value = (g * jax.nn.sigmoid(g) * u).astype(BF16)
        out[...] = value
        for (first, size), whole in zip(cuts[:2], outs[:2]):
            if first <= start < first + size:
                whole[start - first : start - first + count] = value


def hidden_pieces(gate_pre, up_pre, cuts):
    rows, tokens = gate_pre.shape[2:]
    return pl.pallas_call(
        functools.partial(hidden_kernel, cuts),
        in_specs=[pl.BlockSpec(memory_space=pl.ANY)] * 2,
        out_specs=[pl.BlockSpec(memory_space=pltpu.VMEM)] * len(cuts),
        out_shape=[jax.ShapeDtypeStruct((count, tokens), BF16) for _, count in cuts],
        scratch_shapes=[
            pltpu.VMEM((rows, tokens), BF16),
            pltpu.VMEM((rows, tokens), BF16),
            pltpu.SemaphoreType.DMA((2, len(cuts))),
        ],
        compiler_params=pltpu.CompilerParams(vmem_limit_bytes=HIDDEN_LIMIT),
        cost_estimate=pl.CostEstimate(
            flops=16 * rows * tokens,
            bytes_accessed=6 * rows * tokens,
            transcendentals=2 * rows * tokens,
        ),
        name="hidden",
    )(gate_pre, up_pre)


def product(weight, grads):
    return lax.dot_general(weight, grads, (((1,), (1,)), ((), ())), preferred_element_type=F32)


def part_of(weight, rows, z, flips, shard):
    parts = [
        weight[rows, pl.ds(pl.multiple_of((z ^ flip) * shard, 128), shard)] for flip in flips
    ]
    return parts[0] if len(parts) == 1 else jnp.concatenate(parts, axis=1)


def load_kernel(tile, weight_hbm, own_hbm, weight, own, acc_ref, turned, w_sems, own_sem):
    tiles = weight.shape[0] // tile
    z = lax.axis_index("tensor")

    def weight_copy(k):
        rows = pl.ds(pl.multiple_of(k * tile, 16), tile)
        return pltpu.make_async_copy(weight_hbm.at[0, rows], weight.at[rows], w_sems.at[k])

    first = pltpu.make_async_copy(own_hbm.at[0, 0], own, own_sem)
    first.start()
    for k in range(4):
        weight_copy(k).start()
    first.wait()
    turned[...] = own[...].T

    @pl.loop(0, tiles)
    def _(k):
        weight_copy(k).wait()

        @pl.when(k + 4 < tiles)
        def _():
            weight_copy(k + 4).start()

        rows = pl.ds(pl.multiple_of(k * tile, 16), tile)
        acc_ref[rows] = jnp.dot(
            part_of(weight, rows, z, (0,), own.shape[1]),
            turned[...],
            preferred_element_type=F32,
        )


def load_all(weight, out_grad, tile):
    rows, width = weight.shape[1:]
    tokens, shard = out_grad.shape[2:]
    vmem, hbm = (pl.BlockSpec(memory_space=m) for m in (pltpu.VMEM, pl.ANY))
    return pl.pallas_call(
        functools.partial(load_kernel, tile),
        in_specs=[hbm] * 2,
        out_specs=[vmem] * 3,
        out_shape=[
            jax.ShapeDtypeStruct((rows, width), BF16),
            jax.ShapeDtypeStruct((tokens, shard), BF16),
            jax.ShapeDtypeStruct((rows, tokens), F32),
        ],
        scratch_shapes=[
            pltpu.VMEM((shard, tokens), BF16),
            pltpu.SemaphoreType.DMA((rows // tile,)),
            pltpu.SemaphoreType.DMA,
        ],
        compiler_params=pltpu.CompilerParams(vmem_limit_bytes=LOAD_LIMIT),
        cost_estimate=pl.CostEstimate(
            flops=2 * rows * shard * tokens, bytes_accessed=2 * rows * width, transcendentals=0
        ),
        name="load_all",
    )(weight, out_grad)


def grads_kernel(flips, tile, *refs):
    shards, weight, acc_ref, refs = refs[0], refs[1], refs[2], refs[3:]
    turned = refs[-1]
    shard = shards.shape[-1]
    step = pl.program_id(0)

    @pl.when(step == 0)
    def _():
        for k in range(len(flips)):
            turned[k * shard : (k + 1) * shard] = shards[k].T

    rows = pl.ds(pl.multiple_of(step * tile, 16), tile)
    z = lax.axis_index("tensor")
    hidden_grad = acc_ref[rows] + jnp.dot(
        part_of(weight, rows, z, flips, shard), turned[...], preferred_element_type=F32
    )
    if len(refs) == 2:
        refs[0][rows] = hidden_grad
        return
    gate, up, gg_ref, ug_ref = refs[:4]
    g = gate[0, 0, rows].astype(F32)
    u = up[0, 0, rows].astype(F32)
    sig = jax.nn.sigmoid(g)
    gg_ref[0, 0] = (hidden_grad * u * sig * (1.0 + g * (1.0 - sig))).astype(BF16)
    ug_ref[0, 0] = (hidden_grad * g * sig).astype(BF16)


def input_grads(shards, flips, tile, weight, acc, *inputs):
    rows = weight.shape[0]
    n, tokens, shard = shards.shape
    vmem = pl.BlockSpec(memory_space=pltpu.VMEM)
    if inputs:
        out_specs = [pl.BlockSpec((1, 1, tile, tokens), lambda i: (0, 0, i, 0))] * 2
        out_shape = [jax.ShapeDtypeStruct((1, 1, rows, tokens), BF16)] * 2
    else:
        out_specs, out_shape = vmem, jax.ShapeDtypeStruct((rows, tokens), F32)
    return pl.pallas_call(
        functools.partial(grads_kernel, flips, tile),
        grid=(rows // tile,),
        in_specs=[vmem] * (3 + len(inputs)),
        out_specs=out_specs,
        out_shape=out_shape,
        scratch_shapes=[pltpu.VMEM((n * shard, tokens), BF16)],
        compiler_params=pltpu.CompilerParams(vmem_limit_bytes=GRADS_LIMIT),
        cost_estimate=pl.CostEstimate(
            flops=2 * rows * n * shard * tokens,
            bytes_accessed=2 * rows * n * shard,
            transcendentals=0,
        ),
        name="input_grads",
    )(shards, weight, acc, *inputs)


def in_vmem(kernel, operands, shapes):
    vmem = pl.BlockSpec(memory_space=pltpu.VMEM)
    return pl.pallas_call(
        kernel,
        in_specs=[vmem] * len(operands),
        out_specs=[vmem] * len(shapes),
        out_shape=[jax.ShapeDtypeStruct(shape, BF16) for shape in shapes],
        compiler_params=pltpu.CompilerParams(vmem_limit_bytes=4 << 20),
    )(*operands)


def choose_kernel(own_ref, far_ref, mine_ref, theirs_ref, pair_ref):
    same = lax.axis_index("tensor") // 2 == lax.axis_index("dp")
    pair_ref[0] = own_ref[...]
    pair_ref[1] = far_ref[...]

    @pl.when(same)
    def _():
        mine_ref[...] = own_ref[...]
        theirs_ref[...] = far_ref[...]

    @pl.when(jnp.logical_not(same))
    def _():
        mine_ref[...] = far_ref[...]
        theirs_ref[...] = own_ref[...]


def stack_kernel(*refs):
    for k, ref in enumerate(refs[:-1]):
        refs[-1][k] = ref[...]


def cut_kernel(starts, *refs):
    n = len(starts)
    for k, ref in enumerate(refs[:2]):
        for start, out in zip(starts, refs[2 + k * n : 2 + (k + 1) * n]):
            out[...] = ref[start : start + out.shape[0]]


def weight_kernel(scale, starts, steps, tile, *refs):
    hid = refs[:8]
    mine, pair_other, g_other = refs[8:12], refs[12], refs[13]
    out_ref, cols_ref = refs[-2:]
    tokens, shard = mine[0].shape
    step = pl.program_id(0)

    @pl.when(step == 0)
    def _():
        z = lax.axis_index("tensor")
        half = lax.rem(z, 2)
        same = z // 2 == lax.axis_index("dp")

        def columns(place):
            return pl.ds(pl.multiple_of(place * shard, 128), shard)

        for k, ref in enumerate(mine):
            cols_ref[k * tokens : (k + 1) * tokens, columns(half)] = ref[...]
        cols_ref[:tokens, columns(1 - half)] = jnp.where(same, pair_other[0], pair_other[1])
        for k in range(3):
            cols_ref[(k + 1) * tokens : (k + 2) * tokens, columns(1 - half)] = g_other[k]

    for k in range(2):

        @pl.when((step >= k * steps) & (step < (k + 1) * steps))
        def _(k=k):
            at = (step - k * steps) * tile
            parts = [
                ref[pl.ds(pl.multiple_of(start + at, 16), tile)]
                for ref, start in zip(hid[4 * k : 4 * k + 4], starts[4 * k : 4 * k + 4])
            ]
            lhs = jnp.concatenate(parts, axis=1)
            total = jnp.dot(lhs, cols_ref[...], preferred_element_type=F32)
            out_ref[0] = (total * scale).astype(BF16)


def weight_rows(groups, rows, start, count, grads, scale, tile, previous=None):
    half = rows // 2
    tokens, shard = grads[0].shape
    steps = count // tile
    pairs = [pair for group in groups for pair in group]
    operands = [ref for ref, _ in pairs] + list(grads)
    in_specs = [pl.BlockSpec(memory_space=pltpu.VMEM)] * len(operands)
    aliases = {}
    if previous is not None:
        aliases = {len(operands): 0}
        in_specs.append(pl.BlockSpec(memory_space=pl.ANY))
        operands.append(previous)

    def place(i):
        return (0, i // steps * (half // tile) + start // tile + i % steps, 0)

    return pl.pallas_call(
        functools.partial(weight_kernel, scale, [first for _, first in pairs], steps, tile),
        grid=(2 * steps,),
        in_specs=in_specs,
        out_specs=pl.BlockSpec((1, tile, 2 * shard), place),
        out_shape=jax.ShapeDtypeStruct((1, rows, 2 * shard), BF16),
        input_output_aliases=aliases,
        scratch_shapes=[pltpu.VMEM((4 * tokens, 2 * shard), BF16)],
        compiler_params=pltpu.CompilerParams(vmem_limit_bytes=16 << 20),
        cost_estimate=pl.CostEstimate(
            flops=2 * 2 * count * 4 * tokens * 2 * shard,
            bytes_accessed=4 * count * (4 * tokens + 2 * shard),
            transcendentals=0,
        ),
        name="weight_rows",
    )(*operands)


def on_device_quad(out_grad, gate_pre, up_pre, down_weight):
    own = out_grad[0, 0]
    tokens, _ = own.shape
    rows = gate_pre.shape[2]
    half = rows // 2
    pieces = (0, half // 2, half)

    def to_x(value):
        return shifted(value, "dp", 1)

    def to_z(mask):
        return lambda value: crossed(value, "tensor", mask)

    n = len(pieces) - 1
    cuts = [(at + pieces[k], pieces[k + 1] - pieces[k]) for at in (0, half) for k in range(n)]
    hid = hidden_pieces(gate_pre, up_pre, ((0, half), (half, half), *cuts))
    hid_a, hid_b, hid = hid[0], hid[1], hid[2:]
    far = to_z(2)(own)
    a_y = mirrored(hid_a)
    b_x = to_x(hid_b)
    weight, own, acc = load_all(down_weight, out_grad, rows // 8)
    shapes = [own.shape] * 2 + [(2, *own.shape)]
    mine, theirs, pair = in_vmem(choose_kernel, (own, far), shapes)
    g_d = opposite(theirs)
    g_x = to_x(theirs)
    g_y = mirrored(mine)
    pair_other = to_z(1)(pair)
    acc = input_grads(far[None], (2,), rows // 4, weight, acc)
    stacked = in_vmem(stack_kernel, (g_y, g_x, g_d), [(3, *own.shape)])[0]
    g_other = to_z(1)(stacked)
    starts = pieces[:-1]
    shapes = [(end - start, tokens) for start, end in zip(starts, pieces[1:])]
    cuts = in_vmem(functools.partial(cut_kernel, starts), (a_y, b_x), shapes * 2)
    a_d = [to_x(cuts[k]) for k in range(n)]
    b_d = [mirrored(cuts[n + k]) for k in range(n)]
    a_x = [to_x(hid[k]) for k in range(n)]
    b_y = [mirrored(hid[n + k]) for k in range(n)]
    gate_grad, up_grad = input_grads(pair_other, (1, 3), rows // 8, weight, acc, gate_pre, up_pre)
    scale = 32.0 / (2.0 * 2 * tokens)
    out = None
    for k in range(n):
        first = pieces[k]
        a_parts = [(hid_a, first), (a_y, first), (a_x[k], 0), (a_d[k], 0)]
        b_parts = [(hid_b, first), (b_y[k], 0), (b_x, first), (b_d[k], 0)]
        out = weight_rows(
            [a_parts, b_parts],
            rows,
            first,
            pieces[k + 1] - first,
            [mine, g_y, g_x, g_d, pair_other, g_other],
            scale,
            half // 4,
            out,
        )
    return gate_grad, up_grad, out


def on_device(out_grad, gate_pre, up_pre, down_weight):
    n_dp = lax.axis_size("dp")
    n_tensor = lax.axis_size("tensor")
    own_grad = out_grad[0, 0]
    tokens, shard = own_grad.shape
    rows = gate_pre.shape[2]
    if n_dp == 2 and n_tensor == 4 and shard % 128 == 0 and rows % 384 == 0:
        return on_device_quad(out_grad, gate_pre, up_pre, down_weight)
    width = shard * n_tensor
    block = width // n_dp
    pieces = 3
    chunk = rows // pieces
    z = lax.axis_index("tensor")
    x = lax.axis_index("dp")

    grad_full = jnp.zeros((tokens, width), BF16)
    grad_full = lax.dynamic_update_slice(grad_full, own_grad, (0, z * shard))
    for step in range(1, n_tensor):
        got = shifted(own_grad, "tensor", step)
        grad_full = lax.dynamic_update_slice(
            grad_full, got, (0, (z - step) % n_tensor * shard)
        )

    gate = gate_pre[0, 0].astype(F32)
    up = up_pre[0, 0].astype(F32)
    sig = jax.nn.sigmoid(gate)
    hidden = (gate * sig * up).astype(BF16)
    hid = [hidden[i * chunk : (i + 1) * chunk] for i in range(pieces)]
    hid_y = [mirrored(h) for h in hid]
    hid_x = [[shifted(h, "dp", s) for h in hid] for s in range(1, n_dp)]
    hid_d = [
        [
            mirrored(hid_x[s - 1][i]) if i == pieces - 1 else shifted(hid_y[i], "dp", s)
            for i in range(pieces)
        ]
        for s in range(1, n_dp)
    ]
    hidden_grad = product(down_weight[0], grad_full)
    gate_grad = (hidden_grad * up * sig * (1.0 + gate * (1.0 - sig))).astype(BF16)
    up_grad = (hidden_grad * gate * sig).astype(BF16)

    def columns(target):
        return lax.dynamic_slice(grad_full, (0, target * block), (tokens, block))

    cols = [columns(x)]
    cols.append(mirrored(cols[0]))
    for s in range(1, n_dp):
        got = shifted(columns((x + s) % n_dp), "dp", s)
        cols += [got, mirrored(got)]
    cols = jnp.concatenate(cols, axis=0)
    scale = 32.0 / (2.0 * n_dp * tokens)
    out = []
    for i in range(pieces):
        parts = [hid[i], hid_y[i]]
        for s in range(1, n_dp):
            parts += [hid_x[s - 1][i], hid_d[s - 1][i]]
        total = jnp.dot(jnp.concatenate(parts, axis=1), cols, preferred_element_type=F32)
        out.append((total * scale).astype(BF16))
    weight_grad = jnp.concatenate(out, axis=0)
    return gate_grad[None, None], up_grad[None, None], weight_grad[None]


def solution(mesh):
    in_specs = (
        P("pipe", "dp", None, "tensor"),
        P("pipe", "dp", "tensor", None),
        P("pipe", "dp", "tensor", None),
        P("pipe", "tensor", None),
    )
    out_specs = (
        P("pipe", "dp", "tensor", None),
        P("pipe", "dp", "tensor", None),
        P("pipe", "tensor", "dp"),
    )
    return jax.shard_map(
        on_device, mesh=mesh, in_specs=in_specs, out_specs=out_specs, check_vma=False
    )
```

```python
import functools

import jax
import jax.numpy as jnp
from jax import lax
from jax.experimental import pallas as pl
from jax.experimental.pallas import tpu as pltpu
from jax.sharding import PartitionSpec as P


BF16 = jnp.bfloat16
F32 = jnp.float32


def shifted(value, axis, step):
    size = lax.axis_size(axis)
    return lax.ppermute(value, axis, [(i, (i + step) % size) for i in range(size)])


def crossed(value, axis, mask):
    return lax.ppermute(value, axis, [(i, i ^ mask) for i in range(lax.axis_size(axis))])


def mirrored(value):
    return crossed(value, "pipe", lax.axis_size("pipe") // 2)


def opposite(value):
    n_pipe, n_dp = lax.axis_size("pipe"), lax.axis_size("dp")
    mask = n_pipe // 2 * n_dp + 1
    return lax.ppermute(
        value, ("pipe", "dp"), [(i, i ^ mask) for i in range(n_pipe * n_dp)]
    )


HIDDEN_LIMIT = 52 << 20
TILE = 576
LOAD_LIMIT = 30 << 20
GRADS_LIMIT = 6 << 20


def hidden_kernel(cuts, gate_hbm, up_hbm, *refs):
    outs, (gate, up, sems) = refs[:-3], refs[-3:]
    copies = []
    for k, (start, count) in enumerate(cuts[2:]):
        part = pl.ds(start, count)
        pair = [
            pltpu.make_async_copy(gate_hbm.at[0, 0, part], gate.at[part], sems.at[0, k]),
            pltpu.make_async_copy(up_hbm.at[0, 0, part], up.at[part], sems.at[1, k]),
        ]
        for copy in pair:
            copy.start()
        copies.append(pair)
    for (start, count), pair, out in zip(cuts[2:], copies, outs[2:]):
        for copy in pair:
            copy.wait()
        g = gate[start : start + count].astype(F32)
        u = up[start : start + count].astype(F32)
        value = (g * jax.nn.sigmoid(g) * u).astype(BF16)
        out[...] = value
        for (first, size), whole in zip(cuts[:2], outs[:2]):
            if first <= start < first + size:
                whole[start - first : start - first + count] = value


def hidden_pieces(gate_pre, up_pre, cuts):
    rows, tokens = gate_pre.shape[2:]
    return pl.pallas_call(
        functools.partial(hidden_kernel, cuts),
        in_specs=[pl.BlockSpec(memory_space=pl.ANY)] * 2,
        out_specs=[pl.BlockSpec(memory_space=pltpu.VMEM)] * len(cuts),
        out_shape=[jax.ShapeDtypeStruct((count, tokens), BF16) for _, count in cuts],
        scratch_shapes=[
            pltpu.VMEM((rows, tokens), BF16),
            pltpu.VMEM((rows, tokens), BF16),
            pltpu.SemaphoreType.DMA((2, len(cuts))),
        ],
        compiler_params=pltpu.CompilerParams(vmem_limit_bytes=HIDDEN_LIMIT),
        cost_estimate=pl.CostEstimate(
            flops=16 * rows * tokens,
            bytes_accessed=6 * rows * tokens,
            transcendentals=2 * rows * tokens,
        ),
        name="hidden",
    )(gate_pre, up_pre)


def product(weight, grads):
    return lax.dot_general(weight, grads, (((1,), (1,)), ((), ())), preferred_element_type=F32)


def part_of(weight, rows, z, flips, shard):
    parts = [
        weight[rows, pl.ds(pl.multiple_of((z ^ flip) * shard, 128), shard)] for flip in flips
    ]
    return parts[0] if len(parts) == 1 else jnp.concatenate(parts, axis=1)


def load_kernel(tile, weight_hbm, own_hbm, weight, own, acc_ref, turned, w_sems, own_sem):
    tiles = weight.shape[0] // tile
    z = lax.axis_index("tensor")

    def weight_copy(k):
        rows = pl.ds(pl.multiple_of(k * tile, 16), tile)
        return pltpu.make_async_copy(weight_hbm.at[0, rows], weight.at[rows], w_sems.at[k])

    first = pltpu.make_async_copy(own_hbm.at[0, 0], own, own_sem)
    first.start()
    for k in range(4):
        weight_copy(k).start()
    first.wait()
    turned[...] = own[...].T

    @pl.loop(0, tiles)
    def _(k):
        weight_copy(k).wait()

        @pl.when(k + 4 < tiles)
        def _():
            weight_copy(k + 4).start()

        rows = pl.ds(pl.multiple_of(k * tile, 16), tile)
        acc_ref[rows] = jnp.dot(
            part_of(weight, rows, z, (0,), own.shape[1]),
            turned[...],
            preferred_element_type=F32,
        )


def load_all(weight, out_grad, tile):
    rows, width = weight.shape[1:]
    tokens, shard = out_grad.shape[2:]
    vmem, hbm = (pl.BlockSpec(memory_space=m) for m in (pltpu.VMEM, pl.ANY))
    return pl.pallas_call(
        functools.partial(load_kernel, tile),
        in_specs=[hbm] * 2,
        out_specs=[vmem] * 3,
        out_shape=[
            jax.ShapeDtypeStruct((rows, width), BF16),
            jax.ShapeDtypeStruct((tokens, shard), BF16),
            jax.ShapeDtypeStruct((rows, tokens), F32),
        ],
        scratch_shapes=[
            pltpu.VMEM((shard, tokens), BF16),
            pltpu.SemaphoreType.DMA((rows // tile,)),
            pltpu.SemaphoreType.DMA,
        ],
        compiler_params=pltpu.CompilerParams(vmem_limit_bytes=LOAD_LIMIT),
        cost_estimate=pl.CostEstimate(
            flops=2 * rows * shard * tokens, bytes_accessed=2 * rows * width, transcendentals=0
        ),
        name="load_all",
    )(weight, out_grad)


def grads_kernel(flips, tile, *refs):
    shards, weight, acc_ref, refs = refs[0], refs[1], refs[2], refs[3:]
    turned = refs[-1]
    shard = shards.shape[-1]
    step = pl.program_id(0)

    @pl.when(step == 0)
    def _():
        for k in range(len(flips)):
            turned[k * shard : (k + 1) * shard] = shards[k].T

    rows = pl.ds(pl.multiple_of(step * tile, 16), tile)
    z = lax.axis_index("tensor")
    hidden_grad = acc_ref[rows] + jnp.dot(
        part_of(weight, rows, z, flips, shard), turned[...], preferred_element_type=F32
    )
    if len(refs) == 2:
        refs[0][rows] = hidden_grad
        return
    gate, up, gg_ref, ug_ref = refs[:4]
    g = gate[0, 0, rows].astype(F32)
    u = up[0, 0, rows].astype(F32)
    sig = jax.nn.sigmoid(g)
    gg_ref[0, 0] = (hidden_grad * u * sig * (1.0 + g * (1.0 - sig))).astype(BF16)
    ug_ref[0, 0] = (hidden_grad * g * sig).astype(BF16)


def input_grads(shards, flips, tile, weight, acc, *inputs):
    rows = weight.shape[0]
    n, tokens, shard = shards.shape
    vmem = pl.BlockSpec(memory_space=pltpu.VMEM)
    if inputs:
        out_specs = [pl.BlockSpec((1, 1, tile, tokens), lambda i: (0, 0, i, 0))] * 2
        out_shape = [jax.ShapeDtypeStruct((1, 1, rows, tokens), BF16)] * 2
    else:
        out_specs, out_shape = vmem, jax.ShapeDtypeStruct((rows, tokens), F32)
    return pl.pallas_call(
        functools.partial(grads_kernel, flips, tile),
        grid=(rows // tile,),
        in_specs=[vmem] * (3 + len(inputs)),
        out_specs=out_specs,
        out_shape=out_shape,
        scratch_shapes=[pltpu.VMEM((n * shard, tokens), BF16)],
        compiler_params=pltpu.CompilerParams(vmem_limit_bytes=GRADS_LIMIT),
        cost_estimate=pl.CostEstimate(
            flops=2 * rows * n * shard * tokens,
            bytes_accessed=2 * rows * n * shard,
            transcendentals=0,
        ),
        name="input_grads",
    )(shards, weight, acc, *inputs)


def in_vmem(kernel, operands, shapes):
    vmem = pl.BlockSpec(memory_space=pltpu.VMEM)
    return pl.pallas_call(
        kernel,
        in_specs=[vmem] * len(operands),
        out_specs=[vmem] * len(shapes),
        out_shape=[jax.ShapeDtypeStruct(shape, BF16) for shape in shapes],
        compiler_params=pltpu.CompilerParams(vmem_limit_bytes=4 << 20),
    )(*operands)


def choose_kernel(own_ref, far_ref, mine_ref, theirs_ref, pair_ref):
    same = lax.axis_index("tensor") // 2 == lax.axis_index("dp")
    pair_ref[0] = own_ref[...]
    pair_ref[1] = far_ref[...]

    @pl.when(same)
    def _():
        mine_ref[...] = own_ref[...]
        theirs_ref[...] = far_ref[...]

    @pl.when(jnp.logical_not(same))
    def _():
        mine_ref[...] = far_ref[...]
        theirs_ref[...] = own_ref[...]


def stack_kernel(*refs):
    for k, ref in enumerate(refs[:-1]):
        refs[-1][k] = ref[...]


def cut_kernel(starts, *refs):
    n = len(starts)
    for k, ref in enumerate(refs[:2]):
        for start, out in zip(starts, refs[2 + k * n : 2 + (k + 1) * n]):
            out[...] = ref[start : start + out.shape[0]]


def weight_kernel(scale, starts, steps, tile, *refs):
    hid = refs[:8]
    mine, pair_other, g_other = refs[8:12], refs[12], refs[13]
    out_ref, cols_ref = refs[-2:]
    tokens, shard = mine[0].shape
    step = pl.program_id(0)

    @pl.when(step == 0)
    def _():
        z = lax.axis_index("tensor")
        half = lax.rem(z, 2)
        same = z // 2 == lax.axis_index("dp")

        def columns(place):
            return pl.ds(pl.multiple_of(place * shard, 128), shard)

        for k, ref in enumerate(mine):
            cols_ref[k * tokens : (k + 1) * tokens, columns(half)] = ref[...]
        cols_ref[:tokens, columns(1 - half)] = jnp.where(same, pair_other[0], pair_other[1])
        for k in range(3):
            cols_ref[(k + 1) * tokens : (k + 2) * tokens, columns(1 - half)] = g_other[k]

    for k in range(2):

        @pl.when((step >= k * steps) & (step < (k + 1) * steps))
        def _(k=k):
            at = (step - k * steps) * tile
            parts = [
                ref[pl.ds(pl.multiple_of(start + at, 16), tile)]
                for ref, start in zip(hid[4 * k : 4 * k + 4], starts[4 * k : 4 * k + 4])
            ]
            lhs = jnp.concatenate(parts, axis=1)
            total = jnp.dot(lhs, cols_ref[...], preferred_element_type=F32)
            out_ref[0] = (total * scale).astype(BF16)


def weight_rows(groups, rows, start, count, grads, scale, tile, previous=None):
    half = rows // 2
    tokens, shard = grads[0].shape
    steps = count // tile
    pairs = [pair for group in groups for pair in group]
    operands = [ref for ref, _ in pairs] + list(grads)
    in_specs = [pl.BlockSpec(memory_space=pltpu.VMEM)] * len(operands)
    aliases = {}
    if previous is not None:
        aliases = {len(operands): 0}
        in_specs.append(pl.BlockSpec(memory_space=pl.ANY))
        operands.append(previous)

    def place(i):
        return (0, i // steps * (half // tile) + start // tile + i % steps, 0)

    return pl.pallas_call(
        functools.partial(weight_kernel, scale, [first for _, first in pairs], steps, tile),
        grid=(2 * steps,),
        in_specs=in_specs,
        out_specs=pl.BlockSpec((1, tile, 2 * shard), place),
        out_shape=jax.ShapeDtypeStruct((1, rows, 2 * shard), BF16),
        input_output_aliases=aliases,
        scratch_shapes=[pltpu.VMEM((4 * tokens, 2 * shard), BF16)],
        compiler_params=pltpu.CompilerParams(vmem_limit_bytes=16 << 20),
        cost_estimate=pl.CostEstimate(
            flops=2 * 2 * count * 4 * tokens * 2 * shard,
            bytes_accessed=4 * count * (4 * tokens + 2 * shard),
            transcendentals=0,
        ),
        name="weight_rows",
    )(*operands)


def on_device_quad(out_grad, gate_pre, up_pre, down_weight):
    own = out_grad[0, 0]
    tokens, _ = own.shape
    rows = gate_pre.shape[2]
    half = rows // 2
    pieces = (0, half * 2 // 3, half)

    def to_x(value):
        return shifted(value, "dp", 1)

    def to_z(mask):
        return lambda value: crossed(value, "tensor", mask)

    n = len(pieces) - 1
    cuts = [(at + pieces[k], pieces[k + 1] - pieces[k]) for at in (0, half) for k in range(n)]
    hid = hidden_pieces(gate_pre, up_pre, ((0, half), (half, half), *cuts))
    hid_a, hid_b, hid = hid[0], hid[1], hid[2:]
    far = to_z(2)(own)
    a_y = mirrored(hid_a)
    b_x = to_x(hid_b)
    weight, own, acc = load_all(down_weight, out_grad, rows // 8)
    shapes = [own.shape] * 2 + [(2, *own.shape)]
    mine, theirs, pair = in_vmem(choose_kernel, (own, far), shapes)
    g_d = opposite(theirs)
    g_x = to_x(theirs)
    g_y = mirrored(mine)
    pair_other = to_z(1)(pair)
    acc = input_grads(far[None], (2,), rows // 4, weight, acc)
    stacked = in_vmem(stack_kernel, (g_y, g_x, g_d), [(3, *own.shape)])[0]
    g_other = to_z(1)(stacked)
    starts = pieces[:-1]
    shapes = [(end - start, tokens) for start, end in zip(starts, pieces[1:])]
    cuts = in_vmem(functools.partial(cut_kernel, starts), (a_y, b_x), shapes * 2)
    a_d = [to_x(cuts[k]) for k in range(n)]
    b_d = [mirrored(cuts[n + k]) for k in range(n)]
    a_x = [to_x(hid[k]) for k in range(n)]
    b_y = [mirrored(hid[n + k]) for k in range(n)]
    gate_grad, up_grad = input_grads(pair_other, (1, 3), rows // 4, weight, acc, gate_pre, up_pre)
    scale = 32.0 / (2.0 * 2 * tokens)
    out = None
    for k in range(n):
        first = pieces[k]
        a_parts = [(hid_a, first), (a_y, first), (a_x[k], 0), (a_d[k], 0)]
        b_parts = [(hid_b, first), (b_y[k], 0), (b_x, first), (b_d[k], 0)]
        out = weight_rows(
            [a_parts, b_parts],
            rows,
            first,
            pieces[k + 1] - first,
            [mine, g_y, g_x, g_d, pair_other, g_other],
            scale,
            TILE,
            out,
        )
    return gate_grad, up_grad, out


def on_device(out_grad, gate_pre, up_pre, down_weight):
    n_dp = lax.axis_size("dp")
    n_tensor = lax.axis_size("tensor")
    own_grad = out_grad[0, 0]
    tokens, shard = own_grad.shape
    rows = gate_pre.shape[2]
    if n_dp == 2 and n_tensor == 4 and shard % 128 == 0 and rows % 384 == 0:
        return on_device_quad(out_grad, gate_pre, up_pre, down_weight)
    width = shard * n_tensor
    block = width // n_dp
    pieces = 3
    chunk = rows // pieces
    z = lax.axis_index("tensor")
    x = lax.axis_index("dp")

    grad_full = jnp.zeros((tokens, width), BF16)
    grad_full = lax.dynamic_update_slice(grad_full, own_grad, (0, z * shard))
    for step in range(1, n_tensor):
        got = shifted(own_grad, "tensor", step)
        grad_full = lax.dynamic_update_slice(
            grad_full, got, (0, (z - step) % n_tensor * shard)
        )

    gate = gate_pre[0, 0].astype(F32)
    up = up_pre[0, 0].astype(F32)
    sig = jax.nn.sigmoid(gate)
    hidden = (gate * sig * up).astype(BF16)
    hid = [hidden[i * chunk : (i + 1) * chunk] for i in range(pieces)]
    hid_y = [mirrored(h) for h in hid]
    hid_x = [[shifted(h, "dp", s) for h in hid] for s in range(1, n_dp)]
    hid_d = [
        [
            mirrored(hid_x[s - 1][i]) if i == pieces - 1 else shifted(hid_y[i], "dp", s)
            for i in range(pieces)
        ]
        for s in range(1, n_dp)
    ]
    hidden_grad = product(down_weight[0], grad_full)
    gate_grad = (hidden_grad * up * sig * (1.0 + gate * (1.0 - sig))).astype(BF16)
    up_grad = (hidden_grad * gate * sig).astype(BF16)

    def columns(target):
        return lax.dynamic_slice(grad_full, (0, target * block), (tokens, block))

    cols = [columns(x)]
    cols.append(mirrored(cols[0]))
    for s in range(1, n_dp):
        got = shifted(columns((x + s) % n_dp), "dp", s)
        cols += [got, mirrored(got)]
    cols = jnp.concatenate(cols, axis=0)
    scale = 32.0 / (2.0 * n_dp * tokens)
    out = []
    for i in range(pieces):
        parts = [hid[i], hid_y[i]]
        for s in range(1, n_dp):
            parts += [hid_x[s - 1][i], hid_d[s - 1][i]]
        total = jnp.dot(jnp.concatenate(parts, axis=1), cols, preferred_element_type=F32)
        out.append((total * scale).astype(BF16))
    weight_grad = jnp.concatenate(out, axis=0)
    return gate_grad[None, None], up_grad[None, None], weight_grad[None]


def solution(mesh):
    in_specs = (
        P("pipe", "dp", None, "tensor"),
        P("pipe", "dp", "tensor", None),
        P("pipe", "dp", "tensor", None),
        P("pipe", "tensor", None),
    )
    out_specs = (
        P("pipe", "dp", "tensor", None),
        P("pipe", "dp", "tensor", None),
        P("pipe", "tensor", "dp"),
    )
    return jax.shard_map(
        on_device, mesh=mesh, in_specs=in_specs, out_specs=out_specs, check_vma=False
    )
```
